32 devices in a mesh: row: 4 (over y, core), col: 4 (over z), rep: 2 (over x).
Axes of the slice: x: 2, y: 2, z: 4, core: 2. Of those that a mesh axis runs over, the one named last changes fastest.
Arguments:
- precision: float32 [12288, 12288], P('row', 'col'), may hold values from -1 to 4, as said below
- samples: float32 [1024, 12288], P('rep', 'col'), may hold values from -6 to 6
- new_rows: float32 [512, 12288], P(None, 'row'), may hold values from -6 to 6
- ngram_order: int32 [12288], replicated, may hold values from 1 to 3
Outputs:
- updated: float32 [12288, 12288], P('row', ('col', 'rep'))
- residuals: float32 [512, 12288], P('row', ('col', 'rep'))
The draws below stay inside these ranges and needn't reach their ends.
Inputs may be any that keep to these rules, and one draw needn't show every extreme that they name: `precision`: symmetric; diagonal entries from 1 to 4, off-diagonal entries of magnitude at most 9 / sqrt(12288).
All inputs are finite; a program needn't handle non-finite values.
Results may differ from the reference program's by a relative error of at most 0.0003.
Values sent between devices are 32-bit elements; how exact they have to be, the bound alone decides.
A program may use at most 192 MiB of HBM per device.

```python
import math
import jax
import jax.numpy as jnp
from jax import lax

P_SIZE = 12288
NEW = 512
SAMPLES = 1024


def draw_precision(key, part):
    first_key, second_key = jax.random.split(key)
    spread = 3.0 / math.sqrt(P_SIZE)
    entries = jax.random.truncated_normal(first_key, -3.0, 3.0, (P_SIZE, P_SIZE), jnp.float32) * spread
    offdiag = (entries + entries.T) * 0.5
    diagonal = jnp.exp(jax.random.uniform(second_key, (P_SIZE,), jnp.float32, 0.0, math.log(4.0)))
    indices = jnp.arange(P_SIZE)
    return jnp.where(indices[:, None] == indices[None, :], diagonal[None, :], offdiag)


def set_ends(values, own_key, smallest, top_value):
    longest = values.shape.index(max(values.shape))
    spots = []
    for shift in (0, 1):
        where = [jax.random.randint(jax.random.fold_in(own_key, axis), (), 0, length) for axis, length in enumerate(values.shape)]
        where[longest] = (where[longest] + shift) % values.shape[longest]
        spots.append(tuple(where))
    return values.at[spots[0]].set(smallest).at[spots[1]].set(top_value)


def block_levels(own_key, shape, pieces, low, largest):
    factor_of = 1.0
    for position, shards_of in pieces:
        draws = jax.random.uniform(jax.random.fold_in(jax.random.fold_in(own_key, 6), position), (shards_of,), jnp.float32, low / len(pieces), largest / len(pieces))
        factor_of = factor_of * jnp.repeat(jnp.exp(draws), shape[position] // shards_of).reshape((-1,) + (1,) * (len(shape) - 1 - position))
    return factor_of


def gaussian(key, dims, scale, reach, cuts=(), dtype=jnp.bfloat16):
    values = scale * jax.random.normal(key, dims, jnp.float32)
    if cuts:
        values = values * block_levels(key, dims, cuts, -0.22, 0.18)
    return jnp.clip(values, -reach, reach).astype(dtype)


def setup_inputs(seed: int = 0) -> dict:
    arg_keys = jax.random.split(jax.random.key(seed), 5)
    return {
        "precision": draw_precision(jax.random.fold_in(arg_keys[4], 71), 0),
        "samples": gaussian(arg_keys[1], (SAMPLES, P_SIZE), 1.0, 6.0, ((0, 2), (1, 4)), jnp.float32),
        "new_rows": gaussian(arg_keys[2], (NEW, P_SIZE), 1.0, 6.0, ((1, 4),), jnp.float32),
        "ngram_order": set_ends(jax.random.randint(arg_keys[3], (P_SIZE,), 1, 4), jax.random.fold_in(arg_keys[3], 1), 1, 3).astype(jnp.int32),
    }


step_size = 0.25
penalty = 0.08


def contract(left, right, left_dim, right_dim):
    return lax.dot_general(left, right, (((left_dim,), (right_dim,)), ((), ())), preferred_element_type=jnp.float32, precision=lax.Precision.HIGHEST)


def reference(precision, samples, new_rows, ngram_order):
    sample_count = samples.shape[0]
    products = contract(precision, samples, 1, 1)
    diagonal = jnp.diagonal(precision)
    orders = ngram_order.astype(jnp.float32)
    block_size = math.gcd(P_SIZE, 1024)
    offsets = (jnp.arange(P_SIZE // block_size) * block_size).astype(jnp.int32)
    columns = jnp.arange(P_SIZE).astype(jnp.int32)

    def update_block(offset):
        prec_rows = lax.dynamic_slice_in_dim(precision, offset, block_size, 0)
        prod_rows = lax.dynamic_slice_in_dim(products, offset, block_size, 0)
        samp_cols = lax.dynamic_slice_in_dim(samples, offset, block_size, 1)
        symmetric = contract(prod_rows, samples, 1, 0) + contract(samp_cols, products, 0, 1)
        row_ids = offset + jnp.arange(block_size).astype(jnp.int32)
        on_diagonal = row_ids[:, None] == columns[None, :]
        inverse_diag = jnp.where(on_diagonal, 1.0 / jnp.where(on_diagonal, prec_rows, 1.0), 0.0)
        gradient = symmetric / (2.0 * sample_count) - inverse_diag
        stepped = prec_rows - step_size * gradient
        row_orders = lax.dynamic_slice_in_dim(orders, offset, block_size, 0)
        threshold = step_size * penalty * 0.5 * (row_orders[:, None] + orders[None, :])
        shrunk = jnp.sign(stepped) * jnp.maximum(jnp.abs(stepped) - threshold, 0.0)
        return jnp.where(on_diagonal, stepped, shrunk)

    updated = lax.map(update_block, offsets).reshape(P_SIZE, P_SIZE)
    residuals = contract(new_rows, updated, 1, 0) / diagonal[None, :]
    return updated, residuals
```

```python
import jax
import jax.numpy as jnp
from jax import lax
from jax.sharding import PartitionSpec as P

step_size = 0.25
penalty = 0.08
chunks = 2


def contract(left, right, left_dim, right_dim):
    return lax.dot_general(
        left,
        right,
        (((left_dim,), (right_dim,)), ((), ())),
        preferred_element_type=jnp.float32,
        precision=lax.Precision.HIGH,
    )


def swap(array, total):
    return lax.ppermute(array, "rep", [(i, (i + 1) % total) for i in range(total)])


def chain(array, owner, cols, distance, first):
    rows = len(owner)

    def pairs(hop, side):
        return [
            (r * cols + q + side * (hop - 1), r * cols + q + side * hop)
            for r, q in enumerate(owner)
            if 0 <= q + side * hop < cols
        ]

    held = before = lax.optimization_barrier((array, first))[0]
    for hop in range(1, cols):
        before = held
        if hop == 1:
            ahead = lax.ppermute(array, ("row", "col"), pairs(1, 1))
            behind = lax.ppermute(array, ("row", "col"), pairs(1, -1))
            held = jnp.where(distance == 1, ahead, jnp.where(distance == -1, behind, held))
        else:
            both = pairs(hop, 1) + pairs(hop, -1)
            if both:
                got = lax.ppermute(held, ("row", "col"), both)
                held = jnp.where(jnp.abs(distance) == hop, got, held)
    return before, held


def spread(array, source, rows, cols, reps, row_index, own_source):
    offset = rows // 2
    held = array
    holders = {(c, p): [source[c][p]] for c in range(cols) for p in range(reps)}
    while offset >= 1:
        pairs = []
        for (c, p), have in holders.items():
            new = [(r + offset) % rows for r in have]
            pairs += [((a * cols + c) * reps + p, (b * cols + c) * reps + p) for a, b in zip(have, new)]
            holders[(c, p)] = have + new
        got = lax.ppermute(held, ("row", "col", "rep"), pairs)
        away = lax.rem(row_index - own_source + rows, rows)
        held = jnp.where(lax.rem(away, 2 * offset) == offset, got, held)
        offset //= 2
    return held


def per_device(precision, samples, new_rows, ngram_order):
    rows = lax.axis_size("row")
    cols = lax.axis_size("col")
    reps = lax.axis_size("rep")
    r = lax.axis_index("row")
    c = lax.axis_index("col")
    p = lax.axis_index("rep")
    tile_rows, tile_cols = precision.shape
    ratio = rows // cols
    local_k = samples.shape[0]
    sample_count = local_k * reps
    half = tile_cols // reps
    assert reps == 2 and tile_rows % half == 0 and rows & (rows - 1) == 0
    piece = local_k // chunks
    own_begin = p * half
    far_begin = lax.rem(p + 1, reps) * half
    mirror = [(i + rows // 2) % rows for i in range(rows)]
    mirror_index = lax.rem(r + rows // 2, rows)
    begin_row = (c * tile_cols + own_begin)
    own_source = begin_row // tile_rows
    source = [[(i * tile_cols + j * half) // tile_rows for j in range(reps)] for i in range(cols)]
    in_block = lax.rem(begin_row, tile_rows)

    def cut(k):
        return lax.slice_in_dim(samples, k * piece, (k + 1) * piece, axis=0)

    x_cols = [cut(k) for k in range(chunks)]
    partial = [contract(precision, x_cols[k], 1, 1) for k in range(chunks)]

    x_rows, under_way = [], []
    for k in range(chunks):
        if k % 2 == 0:
            index, owner = r, [i // ratio for i in range(rows)]
        else:
            index, owner = mirror_index, [mirror[i] // ratio for i in range(rows)]
        block = lax.dynamic_slice_in_dim(x_cols[k], lax.rem(index, ratio) * tile_rows, tile_rows, 1)
        before, got = chain(block, owner, cols, c - index // ratio, partial[0])
        if k % 2:
            got = lax.ppermute(got, "row", list(enumerate(mirror)))
        x_rows.append(got)
        under_way.append(before)

    prec_half = lax.dynamic_slice_in_dim(precision, own_begin, half, 1)
    row_ids = r * tile_rows + jnp.arange(tile_rows)
    half_ids = c * tile_cols + own_begin + jnp.arange(half)
    on_diagonal = row_ids[:, None] == half_ids[None, :]
    diag = jnp.sum(jnp.where(on_diagonal, prec_half, 0.0), axis=0)
    diag = spread(diag, source, rows, cols, reps, r, own_source)

    x_half_far = [swap(lax.dynamic_slice_in_dim(x, far_begin, half, 1), reps) for x in x_cols]
    products = [lax.psum(partial[0], "col")]
    products[0], *_ = lax.optimization_barrier((products[0], *under_way, *x_half_far))
    for k in range(1, chunks):
        share, products[k - 1] = lax.optimization_barrier((partial[k], products[k - 1]))
        share = lax.psum(share, "col")
        products.append(lax.optimization_barrier((share, diag, *x_rows))[0])

    x_half = [lax.dynamic_slice_in_dim(x, own_begin, half, 1) for x in x_cols]
    x_rows_far = [swap(x, reps) for x in x_rows]

    symmetric = None
    for k in range(chunks):
        mine = products[k]
        far = swap(mine, reps)
        near_cols = lax.dynamic_slice_in_dim(mine, in_block, half, 0)
        far_cols = lax.dynamic_slice_in_dim(far, in_block, half, 0)
        near_cols = spread(near_cols, source, rows, cols, reps, r, own_source)
        far_cols = spread(far_cols, source, rows, cols, reps, r, own_source)
        for term in (
            contract(mine, x_half[k], 1, 0),
            contract(x_rows[k], near_cols, 0, 1),
            contract(far, x_half_far[k], 1, 0),
            contract(x_rows_far[k], far_cols, 0, 1),
        ):
            symmetric = term if symmetric is None else symmetric + term
        symmetric = lax.optimization_barrier(symmetric) if k < chunks - 1 else symmetric

    inverse_diag = jnp.where(on_diagonal, 1.0 / jnp.where(on_diagonal, prec_half, 1.0), 0.0)
    gradient = symmetric / (2.0 * sample_count) - inverse_diag
    stepped = prec_half - step_size * gradient
    orders = ngram_order.astype(jnp.float32)
    order_rows = lax.dynamic_slice_in_dim(orders, r * tile_rows, tile_rows, 0)
    order_cols = lax.dynamic_slice_in_dim(orders, c * tile_cols + own_begin, half, 0)
    threshold = step_size * penalty * 0.5 * (order_rows[:, None] + order_cols[None, :])
    shrunk = jnp.sign(stepped) * jnp.maximum(jnp.abs(stepped) - threshold, 0.0)
    updated = jnp.where(on_diagonal, stepped, shrunk)
    summed = lax.psum_scatter(
        contract(new_rows, updated, 1, 0), "row", scatter_dimension=0, tiled=True
    )
    residuals = summed / diag[None, :]
    return (updated, residuals)


def solution(mesh):
    placed = (P("row", "col"), P("rep", "col"), P(None, "row"), P())
    return jax.shard_map(
        per_device,
        mesh=mesh,
        in_specs=placed,
        out_specs=(P("row", ("col", "rep")), P("row", ("col", "rep"))),
        check_vma=False,
    )
```
